32 devices in a mesh: groups: 2 (over y), row: 4 (over z), col: 4 (over x, core).
Axes of the slice: x: 2, y: 2, z: 4, core: 2. Of those that a mesh axis runs over, the one named last changes fastest.
Arguments:
- tokens: bfloat16 [128, 8192], P(('groups', 'row'), 'col'), parts along dimension 0, may hold values from -6 to 6
- gate_tiles: bfloat16 [256, 4, 12, 128, 256], P(('groups', 'row'), 'col'), parts along dimension 0, may hold values from -0.09375 to 0.09375
- gate_lists: int32 [256, 4, 12], P(('groups', 'row'), 'col'), parts along dimension 0, may hold values from 0 to 15, as said below
- gate_counts: int32 [256, 4], P(('groups', 'row'), 'col'), parts along dimension 0, may hold values from 4 to 12, as said below
- down_tiles: bfloat16 [128, 4, 24, 128, 128], P(('groups', 'row'), 'col'), parts along dimension 0, may hold values from -0.0625 to 0.0625
- down_lists: int32 [128, 4, 24], P(('groups', 'row'), 'col'), parts along dimension 0, may hold values from 0 to 31, as said below
- down_counts: int32 [128, 4], P(('groups', 'row'), 'col'), parts along dimension 0, may hold values from 8 to 24, as said below
Outputs:
- ffn_out: bfloat16 [128, 8192], P(('groups', 'col'), 'row'), parts along dimension 0
The draws below stay inside these ranges and needn't reach their ends.
There are 2 independent parts, one for each index of `groups`. The reference program is written for one: setup_inputs(seed, part) draws one part's arguments, and reference() takes and returns one part's arrays. A program takes and returns all parts, laid end to end along the dimension named above; each array names one. Nothing has to cross between parts.
Inputs may be any that keep to these rules, and one draw needn't show every extreme that they name: `gate_lists`: within each panel the 12 entries are distinct; only the first gate_counts entries are used. `gate_counts`: some panel uses all 12 slots. `down_lists`: within each panel the 24 entries are distinct; only the first down_counts entries are used. `down_counts`: some panel uses all 24 slots.
All inputs are finite; a program needn't handle non-finite values.
Results may differ from the reference program's by a relative error of at most 0.005.
Values may be sent and summed in bfloat16 or wider, within the bound.
No kernel may reach another device: no remote copies, remote signals or barrier semaphores. Data moves between devices by JAX's collectives and lax.ppermute only.
A program may use at most 192 MiB of HBM per device.

```python
import jax
import jax.numpy as jnp
from jax import lax

D = 8192
FW = 16384
BLK = 128
CAP1 = 12
CAP2 = 24
TOKENS = 64
KBT = 64
KBQ = 16
HBT = 128
HBQ = 32
N_COL = 4


def ordered_prefix(key, leading, width, slot_total):
    scores = jax.random.randint(key, leading + (width,), 0, 1 << 20)
    scores = scores * width + jnp.arange(width, dtype=jnp.int32)
    order = jnp.argsort(scores, axis=-1)
    return order[..., :slot_total].astype(jnp.int32)


def panel_counts(key, leading, most):
    drawn = jax.random.randint(jax.random.fold_in(key, 11), leading, most // 3, most + 1)
    flat_counts = drawn.reshape(-1)
    picked = jax.random.randint(jax.random.fold_in(key, 12), (), 0, flat_counts.shape[0])
    flat_counts = jnp.where(jnp.arange(flat_counts.shape[0], dtype=jnp.int32) == picked, most, flat_counts)
    return flat_counts.reshape(leading).astype(jnp.int32)


def draw_gate_lists(key, part):
    return ordered_prefix(jax.random.fold_in(key, 3), (HBT, KBT // KBQ), KBQ, CAP1)


def draw_gate_counts(key, part):
    return panel_counts(jax.random.fold_in(key, 4), (HBT, KBT // KBQ), CAP1)


def draw_down_lists(key, part):
    return ordered_prefix(jax.random.fold_in(key, 5), (KBT, KBT // KBQ), HBQ, CAP2)


def draw_down_counts(key, part):
    return panel_counts(jax.random.fold_in(key, 6), (KBT, KBT // KBQ), CAP2)


def steps_of(stream_key, shape, cuts, least, top_value):
    level = 1.0
    for position, parts in cuts:
        draws = jax.random.uniform(jax.random.fold_in(jax.random.fold_in(stream_key, 6), position), (parts,), jnp.float32, least / len(cuts), top_value / len(cuts))
        level = level * jnp.repeat(jnp.exp(draws), shape[position] // parts).reshape((-1,) + (1,) * (len(shape) - 1 - position))
    return level


def centred(key, dims, spread, reach, pieces=(), held_as=jnp.bfloat16):
    gain = steps_of(key, dims, pieces, -0.22, 0.18) if pieces else 1.0
    array = jax.random.normal(key, dims, jnp.float32) * spread * gain
    return jnp.minimum(jnp.maximum(array, -reach), reach).astype(held_as)


def setup_inputs(seed: int = 0, part: int = 0) -> dict:
    arg_keys = jax.random.split(jax.random.key(seed), 8)
    part_keys = jax.random.split(jax.random.fold_in(arg_keys[7], part), 8)
    return {
        "tokens": centred(part_keys[0], (TOKENS, D), 1.0, 6.0, ((0, 4), (1, 4))),
        "gate_tiles": centred(part_keys[1], (HBT, N_COL, CAP1, BLK, 2 * BLK), (D // 2) ** -0.5, 0.09375, ((0, 4), (1, 4))),
        "gate_lists": draw_gate_lists(jax.random.fold_in(jax.random.fold_in(arg_keys[7], part), 71), part),
        "gate_counts": draw_gate_counts(jax.random.fold_in(jax.random.fold_in(arg_keys[7], part), 71), part),
        "down_tiles": centred(part_keys[4], (KBT, N_COL, CAP2, BLK, BLK), (FW // 2) ** -0.5, 0.0625, ((0, 4), (1, 4))),
        "down_lists": draw_down_lists(jax.random.fold_in(jax.random.fold_in(arg_keys[7], part), 71), part),
        "down_counts": draw_down_counts(jax.random.fold_in(jax.random.fold_in(arg_keys[7], part), 71), part),
    }


def block_product(features, tile_stack, slot_lists, slot_counts, quarter_blocks):
    block = tile_stack.shape[2]
    total_rows = features.shape[0]
    columns = slot_lists.shape[0]
    offsets = (jnp.arange(columns, dtype=jnp.int32) * quarter_blocks)[:, None]
    block_index = (slot_lists + offsets).reshape(-1).astype(jnp.int32)
    slots = jnp.arange(slot_lists.shape[1], dtype=jnp.int32)[None, :]
    keep_mask = (slots < slot_counts[:, None]).reshape(-1).astype(jnp.bfloat16)
    chosen = features[:, block_index, :] * keep_mask[None, :, None]
    return jnp.dot(chosen.reshape(total_rows, -1), tile_stack.reshape(-1, tile_stack.shape[-1]), preferred_element_type=jnp.float32)


def reference(tokens, gate_tiles, gate_lists, gate_counts, down_tiles, down_lists, down_counts):
    block = gate_tiles.shape[3]
    columns = gate_tiles.shape[1]
    total_rows = tokens.shape[0]
    in_blocks = tokens.reshape(total_rows, D // block, block)

    def gate_column(column_args):
        tile_stack, slot_lists, slot_counts = column_args
        return block_product(in_blocks, tile_stack, slot_lists, slot_counts, D // (block * columns))

    gate_up = lax.map(gate_column, (gate_tiles, gate_lists, gate_counts))
    gate_part = gate_up[:, :, :block]
    up_part = gate_up[:, :, block:]
    hidden = (jax.nn.silu(gate_part) * up_part).astype(jnp.bfloat16)
    hidden_blocks = jnp.transpose(hidden, (1, 0, 2))

    def down_column(column_args):
        tile_stack, slot_lists, slot_counts = column_args
        return block_product(hidden_blocks, tile_stack, slot_lists, slot_counts, FW // (block * columns))

    down_out = lax.map(down_column, (down_tiles, down_lists, down_counts))
    return jnp.transpose(down_out, (1, 0, 2)).reshape(total_rows, D).astype(jnp.bfloat16)
```

```python
import functools

import jax
import jax.numpy as jnp
from jax import lax
from jax.experimental import pallas as pl
from jax.experimental.pallas import tpu as pltpu
from jax.sharding import PartitionSpec as P

VMEM = pl.BlockSpec(memory_space=pltpu.VMEM)
SMEM = pl.BlockSpec(memory_space=pltpu.SMEM)
ANY = pl.BlockSpec(memory_space=pl.ANY)


def sparse_kernel(pieces, fan, cap, least, width, x_ref_list, counts, lists, where, tiles, outs, xs, wbuf, acc, sems):
    panels = tiles.shape[0]
    blocks, rows, block = xs.shape
    pairs_least = max(1, least // 2)
    pairs_most = cap // 2

    def pairs_of(panel):
        return jnp.clip((counts[panel, 0] + 1) // 2, pairs_least, pairs_most)

    def copy(panel, pair):
        slots = pl.ds(pair * 2, 2)
        return pltpu.make_async_copy(tiles.at[panel, 0, slots], wbuf.at[panel, slots], sems.at[panel])

    def issue(panel, carry):
        def one(pair, c):
            copy(panel, pair).start()
            return c

        return lax.fori_loop(0, pairs_of(panel), one, carry)

    lax.fori_loop(0, panels, issue, 0)

    for i in range(pieces):
        part_rows = x_ref_list[i].shape[0]
        at = pl.ds(pl.multiple_of(where[i], 16), part_rows)
        for b in range(blocks):
            xs[b, at, :] = x_ref_list[i][:, b * block : (b + 1) * block]

    def work(panel, carry):
        pairs = pairs_of(panel)
        count = counts[panel, 0]

        def one(pair, c):
            copy(panel, pair).wait()
            return c

        lax.fori_loop(0, pairs, one, 0)
        for p in range(pairs_least, pairs_most + 1):

            @pl.when(pairs == p)
            def _(p=p):
                chosen = []
                for s in range(2 * p):
                    x = xs[lists[panel, 0, s]]
                    if s == 2 * p - 1 or s >= least:
                        x = jnp.where(count > s, x, jnp.zeros_like(x))
                    chosen.append(x)
                lhs = jnp.concatenate(chosen, axis=1)
                rhs = wbuf[panel, : 2 * p].reshape(2 * p * block, width)
                acc[...] = jnp.dot(lhs, rhs, preferred_element_type=jnp.float32)

        lanes = pl.ds(pl.multiple_of(panel * width, width), width)
        for k in range(fan):
            part = outs[k].shape[0]
            at = pl.ds(pl.multiple_of(where[pieces + k], 16), part)
            outs[k][:, lanes] = acc[at, :].astype(outs[k].dtype)
        return carry

    lax.fori_loop(0, panels, work, 0)


def sparse_product(xs, offsets, out_offsets, counts, lists, tiles, least):
    panels, _, cap, block, width = tiles.shape
    rows = sum(x.shape[0] for x in xs)
    blocks = xs[0].shape[1] // block
    fan = len(out_offsets)
    pieces = len(xs)
    where = jnp.stack([jnp.asarray(o, jnp.int32) for o in list(offsets) + list(out_offsets)])

    def body(counts_ref, lists_ref, where_ref, *rest):
        x_refs = rest[:pieces]
        tiles_ref = rest[pieces]
        outs = rest[pieces + 1 : pieces + 1 + fan]
        xs_buf, wbuf, acc, sems = rest[pieces + 1 + fan :]
        sparse_kernel(pieces, fan, cap, least, width, x_refs, counts_ref, lists_ref, where_ref, tiles_ref, outs, xs_buf, wbuf, acc, sems)

    return pl.pallas_call(
        body,
        out_shape=[jax.ShapeDtypeStruct((rows // fan, panels * width), jnp.float32 if k == 0 else jnp.bfloat16) for k in range(fan)],
        in_specs=[SMEM, SMEM, SMEM] + [VMEM] * pieces + [ANY],
        out_specs=[VMEM] * fan,
        scratch_shapes=[
            pltpu.VMEM((blocks, rows, block), jnp.bfloat16),
            pltpu.VMEM((panels, cap, block, width), jnp.bfloat16),
            pltpu.VMEM((rows, width), jnp.float32),
            pltpu.SemaphoreType.DMA((panels,)),
        ],
        compiler_params=pltpu.CompilerParams(vmem_limit_bytes=56 * 1024 * 1024),
    )(counts, lists, where, *xs, tiles)


def shifted(x, axis, size, k):
    return lax.ppermute(x, axis, [(i, (i + k) % size) for i in range(size)])


def exchange_sum(parts, axis, size):
    total = parts[0]
    for k in range(1, size):
        total = total + shifted(parts[k], axis, size, k).astype(jnp.float32)
    return total


def local(tokens, gate_tiles, gate_lists, gate_counts, down_tiles, down_lists, down_counts):
    cols, rows = lax.axis_size("col"), lax.axis_size("row")
    row, col = lax.axis_index("row"), lax.axis_index("col")
    hidden_blocks, _, _, block, _ = gate_tiles.shape
    own = tokens.shape[0]
    total = own * rows
    part = total // cols
    part_offsets = [((col + k) % cols) * part for k in range(cols)]

    if rows == cols:
        xs = [tokens] + [shifted(tokens, "row", rows, k) for k in range(1, rows)]
        offsets = [((row + rows - k) % rows) * own for k in range(rows)]
    else:
        xs = [lax.all_gather(tokens, "row", axis=0, tiled=True)]
        offsets = [0]
    sums = sparse_product(xs, offsets, part_offsets, gate_counts, gate_lists, gate_tiles, 4)
    paired = exchange_sum(sums, "col", cols).reshape(part, hidden_blocks, 2, block)
    hidden = (jax.nn.silu(paired[:, :, 0]) * paired[:, :, 1]).astype(jnp.bfloat16).reshape(part, -1)

    if rows == cols:
        hs, h_offsets = [], []
        for k in range(cols):
            pairs = [(r * cols + c, ((c + k) % rows) * cols + r) for r in range(rows) for c in range(cols)]
            hs.append(lax.ppermute(hidden, ("row", "col"), pairs))
            h_offsets.append(((row + rows - k) % rows) * part)
    else:
        every = lax.all_gather(hidden, "row", axis=1, tiled=True).reshape(part, cols, -1)
        every = lax.all_to_all(every, "col", 1, 0, tiled=True)
        hs, h_offsets = [every.reshape(total, -1)], [0]
    outs = sparse_product(hs, h_offsets, part_offsets, down_counts, down_lists, down_tiles, 8)
    return exchange_sum(outs, "col", cols).astype(jnp.bfloat16)


def solution(mesh):
    return jax.shard_map(
        local,
        mesh=mesh,
        in_specs=(
            P(("groups", "row"), "col"),
            P(("groups", "row"), "col", None, None, None),
            P(("groups", "row"), "col", None),
            P(("groups", "row"), "col"),
            P(("groups", "row"), "col", None, None, None),
            P(("groups", "row"), "col", None),
            P(("groups", "row"), "col"),
        ),
        out_specs=P(("groups", "col"), "row"),
        check_vma=False,
    )
```

```python
import math

import jax
import jax.numpy as jnp
from jax import lax
from jax.experimental import pallas as pl
from jax.experimental.pallas import tpu as pltpu
from jax.sharding import PartitionSpec as P

VMEM = pl.BlockSpec(memory_space=pltpu.VMEM)
SMEM = pl.BlockSpec(memory_space=pltpu.SMEM)


class Panels:
    def __init__(self, panels, cap, least, step):
        self.panels, self.cap, self.least = panels, cap, least
        self.group = math.gcd(panels, 4)
        low, high = max(1, least // 2), cap // 2
        self.sizes = sorted({*range(low, high, step), high})
        self.low, self.step = low, step
        self.entries = panels + panels // self.group

    def level(self, count):
        pairs = jnp.clip((count + 1) // 2, self.low, self.cap // 2)
        return (pairs - self.low + self.step - 1) // self.step

    def fill(self, counts_ref, table_ref):
        levels = [self.level(counts_ref[h]) for h in range(self.panels)]
        kinds = len(self.sizes)
        tally = [sum((lv == k).astype(jnp.int32) for lv in levels) for k in range(kinds)]
        at = [jnp.int32(0)]
        for k in range(kinds - 1):
            at.append(at[k] + tally[k])
        for h, lv in enumerate(levels):
            spot = at[0]
            for k in range(1, kinds):
                spot = jnp.where(lv == k, at[k], spot)
            table_ref[spot] = jnp.int32(h)
            at = [a + (lv == k).astype(jnp.int32) for k, a in enumerate(at)]
        for g in range(self.panels // self.group):
            table_ref[self.panels + g] = self.level(counts_ref[table_ref[(g + 1) * self.group - 1]])


def opening():
    def body(out_ref):
        out_ref[...] = jnp.zeros_like(out_ref)

    return pl.pallas_call(
        body,
        out_shape=jax.ShapeDtypeStruct((8, 128), jnp.float32),
        out_specs=VMEM,
        cost_estimate=pl.CostEstimate(flops=1 << 35, transcendentals=0, bytes_accessed=4096),
        compiler_params=pltpu.CompilerParams(vmem_limit_bytes=1 << 20),
        name="opening",
    )()


def plan(kinds, counts, after):
    def body(*refs):
        for kind, counts_ref, table_ref in zip(kinds, refs, refs[len(kinds) + 1 :]):
            kind.fill(counts_ref, table_ref)

    return pl.pallas_call(
        body,
        out_shape=[jax.ShapeDtypeStruct((kind.entries,), jnp.int32) for kind in kinds],
        in_specs=[SMEM] * len(kinds) + [VMEM],
        out_specs=[SMEM] * len(kinds),
        cost_estimate=pl.CostEstimate(flops=1 << 34, transcendentals=0, bytes_accessed=4096),
        compiler_params=pltpu.CompilerParams(vmem_limit_bytes=1 << 20),
        name="plan",
    )(*counts, after)


def product(kind, xs, chunk_of, counts, lists, slots_first, table, tiles, name):
    panels, cap, block, width = tiles.shape
    rows = sum(x.shape[0] for x in xs)
    blocks = xs[0].shape[1] // block
    pieces = len(xs)
    part = rows // 4
    group = kind.group

    def body(counts_ref, lists_ref, table_ref, *rest):
        x_refs = rest[:pieces]
        tiles_ref, kept, sent, x_all = rest[pieces:]
        col = lax.axis_index("col")
        for t in range(4):
            flip = chunk_of(t) ^ col
            spot = (flip & 1) * 2 + flip // 2
            at = pl.ds(pl.multiple_of(spot * part, 16), part)
            for b in range(blocks):
                lanes = slice(b * block, (b + 1) * block)
                x_all[b, at, :] = x_refs[t][:, lanes] if pieces == 4 else x_refs[0][t * part : (t + 1) * part, lanes]

        @pl.loop(0, panels // group)
        def _(g):
            level = table_ref[panels + g]
            members = [table_ref[g * group + u] for u in range(group)]
            for k, pairs in enumerate(kind.sizes):

                @pl.when(level == k)
                def _(pairs=pairs):
                    for panel in members:
                        count = counts_ref[panel]
                        chosen = []
                        for s in range(2 * pairs):
                            x = x_all[lists_ref[s, 0, panel] if slots_first else lists_ref[panel, 0, s]]
                            if s >= kind.least:
                                x = jnp.where(count > s, x, jnp.zeros_like(x))
                            chosen.append(x)
                        lhs = jnp.concatenate(chosen, axis=1)
                        rhs = tiles_ref[panel, : 2 * pairs].reshape(2 * pairs * block, width)
                        sums = jnp.dot(lhs, rhs, preferred_element_type=jnp.float32)
                        lanes = pl.ds(pl.multiple_of(panel * width, width), width)
                        kept[:, lanes] = sums[: rows // 2]
                        sent[:, lanes] = sums[rows // 2 :].astype(sent.dtype)

    return pl.pallas_call(
        body,
        out_shape=[
            jax.ShapeDtypeStruct((rows // 2, panels * width), jnp.float32),
            jax.ShapeDtypeStruct((rows // 2, panels * width), jnp.bfloat16),
        ],
        in_specs=[SMEM] * 3 + [VMEM] * (pieces + 1),
        out_specs=[VMEM, VMEM],
        scratch_shapes=[pltpu.VMEM((blocks, rows, block), jnp.bfloat16)],
        compiler_params=pltpu.CompilerParams(vmem_limit_bytes=(4 << 20) + rows * blocks * block * 4 + rows * width * 8),
        cost_estimate=pl.CostEstimate(flops=2 * rows * tiles.size, transcendentals=0, bytes_accessed=tiles.size * 2),
        name=name,
    )(counts, lists, table, *xs, tiles)


def elementwise(body, shapes, name, *args):
    return pl.pallas_call(
        body,
        out_shape=shapes,
        in_specs=[VMEM] * len(args),
        out_specs=[VMEM] * len(shapes),
        compiler_params=pltpu.CompilerParams(vmem_limit_bytes=4 << 20),
        name=name,
    )(*args)


def add_halves(kept, got):
    half, width = kept.shape[0] // 2, kept.shape[1]

    def body(kept_ref, got_ref, own_ref, send_ref):
        own_ref[...] = kept_ref[:half] + got_ref[:half].astype(jnp.float32)
        send_ref[...] = (kept_ref[half:] + got_ref[half:].astype(jnp.float32)).astype(jnp.bfloat16)

    shapes = [jax.ShapeDtypeStruct((half, width), jnp.float32), jax.ShapeDtypeStruct((half, width), jnp.bfloat16)]
    return elementwise(body, shapes, "add_halves", kept, got)


def swiglu(own, got, block):
    part, width = own.shape
    panels = width // (2 * block)

    def body(own_ref, got_ref, out_ref):
        for h in range(panels):
            lo = h * 2 * block
            gate = own_ref[:, lo : lo + block] + got_ref[:, lo : lo + block].astype(jnp.float32)
            up = own_ref[:, lo + block : lo + 2 * block] + got_ref[:, lo + block : lo + 2 * block].astype(jnp.float32)
            out_ref[:, h * block : (h + 1) * block] = (gate / (1.0 + jnp.exp(-gate)) * up).astype(jnp.bfloat16)

    return elementwise(body, [jax.ShapeDtypeStruct((part, width // 2), jnp.bfloat16)], "swiglu", own, got)[0]


def last_sum(own, got):
    def body(own_ref, got_ref, out_ref):
        out_ref[...] = (own_ref[...] + got_ref[...].astype(jnp.float32)).astype(jnp.bfloat16)

    return elementwise(body, [jax.ShapeDtypeStruct(own.shape, jnp.bfloat16)], "last_sum", own, got)[0]


def flipped(x, bit):
    return lax.ppermute(x, "col", [(i, i ^ bit) for i in range(4)])


def local(tokens, gate_tiles, gate_lists, gate_counts, down_tiles, down_lists, down_counts):
    cols, rows = lax.axis_size("col"), lax.axis_size("row")
    assert cols == 4
    block = gate_tiles.shape[3]
    total = tokens.shape[0] * rows
    part = total // cols
    square = rows == cols

    gate_kind = Panels(gate_tiles.shape[0], gate_tiles.shape[2], 4, 1)
    down_kind = Panels(down_tiles.shape[0], down_tiles.shape[2], 8, 2)
    gate_used, down_used = gate_counts.reshape(-1), down_counts.reshape(-1)

    def chunk_of(k):
        return lax.rem(lax.axis_index("row") + (rows - k), rows) if square else k

    tokens, opened = lax.optimization_barrier((tokens, opening()))
    if square:
        xs = [tokens] + [lax.ppermute(tokens, "row", [(i, (i + k) % rows) for i in range(rows)]) for k in range(1, rows)]
    else:
        xs = [lax.all_gather(tokens, "row", axis=0, tiled=True)]
    gate_table, down_table = plan([gate_kind, down_kind], [gate_used, down_used], opened)

    kept, sent = product(
        gate_kind, xs, chunk_of, gate_used, jnp.transpose(gate_lists, (2, 1, 0)), True, gate_table, gate_tiles[:, 0], "gate_up"
    )
    summed, crossing = add_halves(kept, flipped(sent, 1))
    hidden = swiglu(summed, flipped(crossing, 2), block)

    if square:
        hs = [
            lax.ppermute(
                hidden, ("row", "col"), [(r * cols + c, ((c + k) % rows) * cols + r) for r in range(rows) for c in range(cols)]
            )
            for k in range(cols)
        ]
    else:
        every = lax.all_gather(hidden, "row", axis=1, tiled=True).reshape(part, cols, -1)
        every = lax.all_to_all(every, "col", 1, 0, tiled=True)
        hs = [every.reshape(total, -1)]
    kept, sent = product(down_kind, hs, chunk_of, down_used, down_lists, False, down_table, down_tiles[:, 0], "down")
    summed, crossing = add_halves(kept, flipped(sent, 1))
    return last_sum(summed, flipped(crossing, 2))


def solution(mesh):
    return jax.shard_map(
        local,
        mesh=mesh,
        in_specs=(
            P(("groups", "row"), "col"),
            P(("groups", "row"), "col", None, None, None),
            P(("groups", "row"), "col", None),
            P(("groups", "row"), "col"),
            P(("groups", "row"), "col", None, None, None),
            P(("groups", "row"), "col", None),
            P(("groups", "row"), "col"),
        ),
        out_specs=P(("groups", "col"), "row"),
        check_vma=False,
    )
```

```python
import math

import jax
import jax.numpy as jnp
from jax import lax
from jax.experimental import pallas as pl
from jax.experimental.pallas import tpu as pltpu
from jax.sharding import PartitionSpec as P

VMEM = pl.BlockSpec(memory_space=pltpu.VMEM)
SMEM = pl.BlockSpec(memory_space=pltpu.SMEM)
EARLY = (1, 3)


class Panels:
    def __init__(self, first, panels, cap, least, step):
        self.first, self.panels, self.cap, self.least = first, panels, cap, least
        self.group = math.gcd(panels, 4)
        low, high = max(1, least // 2), cap // 2
        self.sizes = sorted({*range(low, high, step), high})
        self.low, self.step = low, step
        self.entries = panels + panels // self.group

    def level(self, count):
        pairs = jnp.clip((count + 1) // 2, self.low, self.cap // 2)
        return (pairs - self.low + self.step - 1) // self.step

    def fill(self, counts_ref, table_ref):
        levels = [self.level(counts_ref[self.first + h]) for h in range(self.panels)]
        kinds = len(self.sizes)
        tally = [sum((lv == k).astype(jnp.int32) for lv in levels) for k in range(kinds)]
        at = [jnp.int32(0)]
        for k in range(kinds - 1):
            at.append(at[k] + tally[k])
        for h, lv in enumerate(levels):
            spot = at[0]
            for k in range(1, kinds):
                spot = jnp.where(lv == k, at[k], spot)
            table_ref[spot] = jnp.int32(self.first + h)
            at = [a + (lv == k).astype(jnp.int32) for k, a in enumerate(at)]
        for g in range(self.panels // self.group):
            table_ref[self.panels + g] = self.level(counts_ref[table_ref[(g + 1) * self.group - 1]])


def opening():
    def body(out_ref):
        out_ref[...] = jnp.zeros_like(out_ref)

    return pl.pallas_call(
        body,
        out_shape=jax.ShapeDtypeStruct((8, 128), jnp.float32),
        out_specs=VMEM,
        cost_estimate=pl.CostEstimate(flops=1 << 35, transcendentals=0, bytes_accessed=4096),
        compiler_params=pltpu.CompilerParams(vmem_limit_bytes=1 << 20),
        name="opening",
    )()


def plan(kinds, counts, after):
    def body(*refs):
        for kind, counts_ref, table_ref in zip(kinds, refs, refs[len(kinds) + 1 :]):
            kind.fill(counts_ref, table_ref)

    return pl.pallas_call(
        body,
        out_shape=[jax.ShapeDtypeStruct((kind.entries,), jnp.int32) for kind in kinds],
        in_specs=[SMEM] * len(kinds) + [VMEM],
        out_specs=[SMEM] * len(kinds),
        cost_estimate=pl.CostEstimate(flops=1 << 34, transcendentals=0, bytes_accessed=4096),
        compiler_params=pltpu.CompilerParams(vmem_limit_bytes=1 << 20),
        name="plan",
    )(*counts, after)


def product(kind, xs, chunk_of, counts, lists, slots_first, table, tiles, name):
    _, _, block, width = tiles.shape
    panels, group = kind.panels, kind.group
    pieces = len(xs)
    rows = sum(lanes[0].shape[0] for lanes in xs)
    blocks = sum(x.shape[1] for x in xs[0]) // block
    part = rows // 4

    def body(counts_ref, lists_ref, table_ref, *rest):
        x_refs = list(rest[:-4])
        tiles_ref, kept, sent, x_all = rest[-4:]
        col = lax.axis_index("col")
        grouped = [[x_refs.pop(0) for _ in lanes] for lanes in xs]
        for t in range(4):
            flip = chunk_of(t) ^ col
            spot = (flip & 1) * 2 + flip // 2
            at = pl.ds(pl.multiple_of(spot * part, 16), part)
            lead = slice(0, part) if pieces == 4 else slice(t * part, (t + 1) * part)
            b = 0
            for ref in grouped[t if pieces == 4 else 0]:
                for lo in range(0, ref.shape[1], block):
                    x_all[b, at, :] = ref[lead, lo : lo + block]
                    b += 1

        @pl.loop(0, panels // group)
        def _(g):
            level = table_ref[panels + g]
            members = [table_ref[g * group + u] for u in range(group)]
            for k, pairs in enumerate(kind.sizes):

                @pl.when(level == k)
                def _(pairs=pairs):
                    for panel in members:
                        count = counts_ref[panel]
                        chosen = []
                        for s in range(2 * pairs):
                            x = x_all[lists_ref[s, 0, panel] if slots_first else lists_ref[panel, 0, s]]
                            if s >= kind.least:
                                x = jnp.where(count > s, x, jnp.zeros_like(x))
                            chosen.append(x)
                        lhs = jnp.concatenate(chosen, axis=1)
                        rhs = tiles_ref[panel, : 2 * pairs].reshape(2 * pairs * block, width)
                        sums = jnp.dot(lhs, rhs, preferred_element_type=jnp.float32)
                        lanes = pl.ds(pl.multiple_of((panel - kind.first) * width, width), width)
                        kept[:, lanes] = sums[: rows // 2]
                        sent[:, lanes] = sums[rows // 2 :].astype(sent.dtype)

    return pl.pallas_call(
        body,
        out_shape=[
            jax.ShapeDtypeStruct((rows // 2, panels * width), jnp.float32),
            jax.ShapeDtypeStruct((rows // 2, panels * width), jnp.bfloat16),
        ],
        in_specs=[SMEM] * 3 + [VMEM] * (sum(len(lanes) for lanes in xs) + 1),
        out_specs=[VMEM, VMEM],
        scratch_shapes=[pltpu.VMEM((blocks, rows, block), jnp.bfloat16)],
        compiler_params=pltpu.CompilerParams(vmem_limit_bytes=(4 << 20) + rows * blocks * block * 4 + rows * width * 8),
        cost_estimate=pl.CostEstimate(flops=2 * rows * panels * tiles[0].size, transcendentals=0, bytes_accessed=panels * tiles[0].size * 2),
        name=name,
    )(counts, lists, table, *[x for lanes in xs for x in lanes], tiles)


def elementwise(body, shapes, name, *args):
    return pl.pallas_call(
        body,
        out_shape=shapes,
        in_specs=[VMEM] * len(args),
        out_specs=[VMEM] * len(shapes),
        compiler_params=pltpu.CompilerParams(vmem_limit_bytes=4 << 20),
        name=name,
    )(*args)


def add_halves(kept, got):
    half, width = kept.shape[0] // 2, kept.shape[1]

    def body(kept_ref, got_ref, own_ref, send_ref):
        own_ref[...] = kept_ref[:half] + got_ref[:half].astype(jnp.float32)
        send_ref[...] = (kept_ref[half:] + got_ref[half:].astype(jnp.float32)).astype(jnp.bfloat16)

    shapes = [jax.ShapeDtypeStruct((half, width), jnp.float32), jax.ShapeDtypeStruct((half, width), jnp.bfloat16)]
    return elementwise(body, shapes, "add_halves", kept, got)


def swiglu(own, got, block, ahead=None):
    part, width = own.shape
    lead = 0 if ahead is None else ahead.shape[1]

    def body(own_ref, got_ref, *rest):
        for lo in range(0, width, 2 * block):
            gate = own_ref[:, lo : lo + block] + got_ref[:, lo : lo + block].astype(jnp.float32)
            up = own_ref[:, lo + block : lo + 2 * block] + got_ref[:, lo + block : lo + 2 * block].astype(jnp.float32)
            units = (gate / (1.0 + jnp.exp(-gate)) * up).astype(jnp.bfloat16)
            if lead:
                rest[1][:, lo // 2 : lo // 2 + block] = units
                rest[2][:, lead + lo // 2 : lead + lo // 2 + block] = units
            else:
                rest[0][:, lo // 2 : lo // 2 + block] = units
        if lead:
            rest[2][:, :lead] = rest[0][...]

    shapes = [jax.ShapeDtypeStruct((part, width // 2), jnp.bfloat16)]
    if lead:
        return elementwise(body, shapes + [jax.ShapeDtypeStruct((part, lead + width // 2), jnp.bfloat16)], "swiglu", own, got, ahead)
    return elementwise(body, shapes, "swiglu", own, got)[0]


def last_sum(own, got):
    def body(own_ref, got_ref, out_ref):
        out_ref[...] = (own_ref[...] + got_ref[...].astype(jnp.float32)).astype(jnp.bfloat16)

    return elementwise(body, [jax.ShapeDtypeStruct(own.shape, jnp.bfloat16)], "last_sum", own, got)[0]


def flipped(x, bit):
    return lax.ppermute(x, "col", [(i, i ^ bit) for i in range(4)])


def local(tokens, gate_tiles, gate_lists, gate_counts, down_tiles, down_lists, down_counts):
    cols, rows = lax.axis_size("col"), lax.axis_size("row")
    assert cols == 4
    block = gate_tiles.shape[3]
    total = tokens.shape[0] * rows
    part = total // cols
    square = rows == cols

    halves = 2 if gate_tiles.shape[0] % 2 == 0 else 1
    each = gate_tiles.shape[0] // halves
    gate_kinds = [Panels(i * each, each, gate_tiles.shape[2], 4, 1) for i in range(halves)]
    down_kind = Panels(0, down_tiles.shape[0], down_tiles.shape[2], 8, 2)
    gate_used, down_used = gate_counts.reshape(-1), down_counts.reshape(-1)
    slots = jnp.transpose(gate_lists, (2, 1, 0))

    def chunk_of(k):
        return lax.rem(lax.axis_index("row") + (rows - k), rows) if square else k

    tokens, opened = lax.optimization_barrier((tokens, opening()))
    if square:
        xs = [[tokens]] + [[lax.ppermute(tokens, "row", [(i, (i + k) % rows) for i in range(rows)])] for k in range(1, rows)]
    else:
        xs = [[lax.all_gather(tokens, "row", axis=0, tiled=True)]]
    *gate_tables, down_table = plan([*gate_kinds, down_kind], [gate_used] * halves + [down_used], opened)

    sums = [
        product(kind, xs, chunk_of, gate_used, slots, True, table, gate_tiles[:, 0], "gate_up")
        for kind, table in zip(gate_kinds, gate_tables)
    ]
    pairs = []
    for kept, sent in sums:
        summed, crossing = add_halves(kept, flipped(sent, 1))
        pairs.append((summed, flipped(crossing, 2)))
    hidden = swiglu(*pairs[0], block)
    if len(pairs) > 1:
        first = hidden
        second, hidden = swiglu(*pairs[1], block, first)

    if square:

        def spread(x, k):
            there = [(r * cols + c, ((c + k) % rows) * cols + r) for r in range(rows) for c in range(cols)]
            return lax.ppermute(x, ("row", "col"), there)

        early = EARLY if len(pairs) > 1 else ()
        hs = [[spread(first, k), spread(second, k)] if k in early else [spread(hidden, k)] for k in range(cols)]
    else:
        every = lax.all_gather(hidden, "row", axis=1, tiled=True).reshape(part, cols, -1)
        every = lax.all_to_all(every, "col", 1, 0, tiled=True)
        hs = [[every.reshape(total, -1)]]
    kept, sent = product(down_kind, hs, chunk_of, down_used, down_lists, False, down_table, down_tiles[:, 0], "down")
    summed, crossing = add_halves(kept, flipped(sent, 1))
    return last_sum(summed, flipped(crossing, 2))


def solution(mesh):
    return jax.shard_map(
        local,
        mesh=mesh,
        in_specs=(
            P(("groups", "row"), "col"),
            P(("groups", "row"), "col", None, None, None),
            P(("groups", "row"), "col", None),
            P(("groups", "row"), "col"),
            P(("groups", "row"), "col", None, None, None),
            P(("groups", "row"), "col", None),
            P(("groups", "row"), "col"),
        ),
        out_specs=P(("groups", "col"), "row"),
        check_vma=False,
    )
```

```python
import math

import jax
import jax.numpy as jnp
from jax import lax
from jax.experimental import pallas as pl
from jax.experimental.pallas import tpu as pltpu
from jax.sharding import PartitionSpec as P

VMEM = pl.BlockSpec(memory_space=pltpu.VMEM)
SMEM = pl.BlockSpec(memory_space=pltpu.SMEM)
EARLY = (1, 3)


class Panels:
    def __init__(self, first, panels, cap, least, step):
        self.first, self.panels, self.cap, self.least = first, panels, cap, least
        self.group = math.gcd(panels, 4)
        low, high = max(1, least // 2), cap // 2
        self.sizes = sorted({*range(low, high, step), high})
        self.low, self.step = low, step
        self.entries = panels + panels // self.group

    def level(self, count):
        pairs = jnp.clip((count + 1) // 2, self.low, self.cap // 2)
        return (pairs - self.low + self.step - 1) // self.step

    def fill(self, counts_ref, table_ref):
        levels = [self.level(counts_ref[self.first + h]) for h in range(self.panels)]
        kinds = len(self.sizes)
        tally = [sum((lv == k).astype(jnp.int32) for lv in levels) for k in range(kinds)]
        at = [jnp.int32(0)]
        for k in range(kinds - 1):
            at.append(at[k] + tally[k])
        for h, lv in enumerate(levels):
            spot = at[0]
            for k in range(1, kinds):
                spot = jnp.where(lv == k, at[k], spot)
            table_ref[spot] = jnp.int32(self.first + h)
            at = [a + (lv == k).astype(jnp.int32) for k, a in enumerate(at)]
        for g in range(self.panels // self.group):
            table_ref[self.panels + g] = self.level(counts_ref[table_ref[(g + 1) * self.group - 1]])


def opening():
    def body(out_ref):
        out_ref[...] = jnp.zeros_like(out_ref)

    return pl.pallas_call(
        body,
        out_shape=jax.ShapeDtypeStruct((8, 128), jnp.float32),
        out_specs=VMEM,
        cost_estimate=pl.CostEstimate(flops=1 << 35, transcendentals=0, bytes_accessed=4096),
        compiler_params=pltpu.CompilerParams(vmem_limit_bytes=1 << 20),
        name="opening",
    )()


def plan(kinds, counts, after):
    def body(*refs):
        for kind, counts_ref, table_ref in zip(kinds, refs, refs[len(kinds) + 1 :]):
            kind.fill(counts_ref, table_ref)

    return pl.pallas_call(
        body,
        out_shape=[jax.ShapeDtypeStruct((kind.entries,), jnp.int32) for kind in kinds],
        in_specs=[SMEM] * len(kinds) + [VMEM],
        out_specs=[SMEM] * len(kinds),
        cost_estimate=pl.CostEstimate(flops=1 << 10, transcendentals=0, bytes_accessed=4096),
        compiler_params=pltpu.CompilerParams(vmem_limit_bytes=1 << 20),
        name="plan",
    )(*counts, after)


def product(kind, xs, chunk_of, counts, lists, slots_first, table, tiles, name, outs):
    _, _, block, width = tiles.shape
    panels, group = kind.panels, kind.group
    pieces = len(xs)
    rows = sum(lanes[0].shape[0] for lanes in xs)
    blocks = sum(x.shape[1] for x in xs[0]) // block
    part = rows // 4

    def body(counts_ref, lists_ref, table_ref, *rest):
        x_refs = list(rest[: -2 - len(outs)])
        tiles_ref, x_all = rest[-2 - len(outs)], rest[-1]
        out_refs = rest[-1 - len(outs) : -1]
        col = lax.axis_index("col")
        grouped = [[x_refs.pop(0) for _ in lanes] for lanes in xs]
        for t in range(4):
            flip = chunk_of(t) ^ col
            spot = (flip & 1) * 2 + flip // 2
            at = pl.ds(pl.multiple_of(spot * part, 16), part)
            lead = slice(0, part) if pieces == 4 else slice(t * part, (t + 1) * part)
            b = 0
            for ref in grouped[t if pieces == 4 else 0]:
                for lo in range(0, ref.shape[1], block):
                    x_all[b, at, :] = ref[lead, lo : lo + block]
                    b += 1

        @pl.loop(0, panels // group)
        def _(g):
            level = table_ref[panels + g]
            members = [table_ref[g * group + u] for u in range(group)]
            for k, pairs in enumerate(kind.sizes):

                @pl.when(level == k)
                def _(pairs=pairs):
                    for panel in members:
                        count = counts_ref[panel]
                        chosen = []
                        for s in range(2 * pairs):
                            x = x_all[lists_ref[s, 0, panel] if slots_first else lists_ref[panel, 0, s]]
                            if s >= kind.least:
                                x = jnp.where(count > s, x, jnp.zeros_like(x))
                            chosen.append(x)
                        lhs = jnp.concatenate(chosen, axis=1)
                        rhs = tiles_ref[panel, : 2 * pairs].reshape(2 * pairs * block, width)
                        sums = jnp.dot(lhs, rhs, preferred_element_type=jnp.float32)
                        lanes = pl.ds(pl.multiple_of((panel - kind.first) * width, width), width)
                        at = 0
                        for out_ref in out_refs:
                            size = out_ref.shape[0]
                            out_ref[:, lanes] = sums[at : at + size].astype(out_ref.dtype)
                            at += size

    return pl.pallas_call(
        body,
        out_shape=[jax.ShapeDtypeStruct((n * part, panels * width), dtype) for n, dtype in outs],
        in_specs=[SMEM] * 3 + [VMEM] * (sum(len(lanes) for lanes in xs) + 1),
        out_specs=[VMEM] * len(outs),
        scratch_shapes=[pltpu.VMEM((blocks, rows, block), jnp.bfloat16)],
        compiler_params=pltpu.CompilerParams(vmem_limit_bytes=(4 << 20) + rows * blocks * block * 4 + rows * width * 8),
        cost_estimate=pl.CostEstimate(flops=2 * rows * panels * tiles[0].size, transcendentals=0, bytes_accessed=panels * tiles[0].size * 2),
        name=name,
    )(counts, lists, table, *[x for lanes in xs for x in lanes], tiles)


def elementwise(body, shapes, name, *args):
    return pl.pallas_call(
        body,
        out_shape=shapes,
        in_specs=[VMEM] * len(args),
        out_specs=[VMEM] * len(shapes),
        compiler_params=pltpu.CompilerParams(vmem_limit_bytes=4 << 20),
        name=name,
    )(*args)


def add_halves(kept, got):
    half, width = kept.shape[0] // 2, kept.shape[1]

    def body(kept_ref, got_ref, own_ref, send_ref):
        own_ref[...] = kept_ref[:half] + got_ref[:half].astype(jnp.float32)
        send_ref[...] = (kept_ref[half:] + got_ref[half:].astype(jnp.float32)).astype(jnp.bfloat16)

    shapes = [jax.ShapeDtypeStruct((half, width), jnp.float32), jax.ShapeDtypeStruct((half, width), jnp.bfloat16)]
    return elementwise(body, shapes, "add_halves", kept, got)


def swiglu(own, got, block, ahead=None):
    part, width = own.shape
    lead = 0 if ahead is None else ahead.shape[1]

    def body(own_ref, got_ref, *rest):
        for lo in range(0, width, 2 * block):
            gate = own_ref[:, lo : lo + block] + got_ref[:, lo : lo + block].astype(jnp.float32)
            up = own_ref[:, lo + block : lo + 2 * block] + got_ref[:, lo + block : lo + 2 * block].astype(jnp.float32)
            units = (gate / (1.0 + jnp.exp(-gate)) * up).astype(jnp.bfloat16)
            if lead:
                rest[1][:, lo // 2 : lo // 2 + block] = units
                rest[2][:, lead + lo // 2 : lead + lo // 2 + block] = units
            else:
                rest[0][:, lo // 2 : lo // 2 + block] = units
        if lead:
            rest[2][:, :lead] = rest[0][...]

    shapes = [jax.ShapeDtypeStruct((part, width // 2), jnp.bfloat16)]
    if lead:
        return elementwise(body, shapes + [jax.ShapeDtypeStruct((part, lead + width // 2), jnp.bfloat16)], "swiglu", own, got, ahead)
    return elementwise(body, shapes, "swiglu", own, got)[0]


def last_sum(own, *got):
    def body(own_ref, *rest):
        total = own_ref[...]
        for got_ref in rest[:-1]:
            total = total + got_ref[...].astype(jnp.float32)
        rest[-1][...] = total.astype(jnp.bfloat16)

    return elementwise(body, [jax.ShapeDtypeStruct(own.shape, jnp.bfloat16)], "last_sum", own, *got)[0]


def flipped(x, bit):
    return lax.ppermute(x, "col", [(i, i ^ bit) for i in range(4)])


def local(tokens, gate_tiles, gate_lists, gate_counts, down_tiles, down_lists, down_counts):
    cols, rows = lax.axis_size("col"), lax.axis_size("row")
    assert cols == 4
    block = gate_tiles.shape[3]
    total = tokens.shape[0] * rows
    part = total // cols
    square = rows == cols

    halves = 2 if gate_tiles.shape[0] % 2 == 0 else 1
    each = gate_tiles.shape[0] // halves
    gate_kinds = [Panels(i * each, each, gate_tiles.shape[2], 4, 1) for i in range(halves)]
    down_kind = Panels(0, down_tiles.shape[0], down_tiles.shape[2], 8, 2)
    gate_used, down_used = gate_counts.reshape(-1), down_counts.reshape(-1)
    slots = jnp.transpose(gate_lists, (2, 1, 0))

    def chunk_of(k):
        return lax.rem(lax.axis_index("row") + (rows - k), rows) if square else k

    tokens, opened = lax.optimization_barrier((tokens, opening()))
    if square:
        xs = [[tokens]] + [[lax.ppermute(tokens, "row", [(i, (i + k) % rows) for i in range(rows)])] for k in range(1, rows)]
    else:
        xs = [[lax.all_gather(tokens, "row", axis=0, tiled=True)]]
    *gate_tables, down_table = plan([*gate_kinds, down_kind], [gate_used] * halves + [down_used], opened)

    pairwise = [(2, jnp.float32), (2, jnp.bfloat16)]
    sums = [
        product(kind, xs, chunk_of, gate_used, slots, True, table, gate_tiles[:, 0], "gate_up", pairwise)
        for kind, table in zip(gate_kinds, gate_tables)
    ]
    pairs = []
    for kept, sent in sums:
        summed, crossing = add_halves(kept, flipped(sent, 1))
        pairs.append((summed, flipped(crossing, 2)))
    hidden = swiglu(*pairs[0], block)
    if len(pairs) > 1:
        first = hidden
        second, hidden = swiglu(*pairs[1], block, first)

    if square:

        def spread(x, k):
            there = [(r * cols + c, ((c + k) % rows) * cols + r) for r in range(rows) for c in range(cols)]
            return lax.ppermute(x, ("row", "col"), there)

        early = EARLY if len(pairs) > 1 else ()
        hs = [[spread(first, k), spread(second, k)] if k in early else [spread(hidden, k)] for k in range(cols)]
    else:
        every = lax.all_gather(hidden, "row", axis=1, tiled=True).reshape(part, cols, -1)
        every = lax.all_to_all(every, "col", 1, 0, tiled=True)
        hs = [[every.reshape(total, -1)]]
    straight = [(1, jnp.float32)] + [(1, jnp.bfloat16)] * 3
    own, *away = product(down_kind, hs, chunk_of, down_used, down_lists, False, down_table, down_tiles[:, 0], "down", straight)
    return last_sum(own, *[flipped(x, bit) for x, bit in zip(away, (2, 1, 3))])


def solution(mesh):
    return jax.shard_map(
        local,
        mesh=mesh,
        in_specs=(
            P(("groups", "row"), "col"),
            P(("groups", "row"), "col", None, None, None),
            P(("groups", "row"), "col", None),
            P(("groups", "row"), "col"),
            P(("groups", "row"), "col", None, None, None),
            P(("groups", "row"), "col", None),
            P(("groups", "row"), "col"),
        ),
        out_specs=P(("groups", "col"), "row"),
        check_vma=False,
    )
```

```python
import math

import jax
import jax.numpy as jnp
from jax import lax
from jax.experimental import pallas as pl
from jax.experimental.pallas import tpu as pltpu
from jax.sharding import PartitionSpec as P

VMEM = pl.BlockSpec(memory_space=pltpu.VMEM)
SMEM = pl.BlockSpec(memory_space=pltpu.SMEM)
EARLY = (1, 3)


class Panels:
    def __init__(self, first, panels, cap, least, step):
        self.first, self.panels, self.cap, self.least = first, panels, cap, least
        self.group = math.gcd(panels, 4)
        low, high = max(1, least // 2), cap // 2
        self.sizes = sorted({*range(low, high, step), high})
        self.low, self.step = low, step
        self.entries = panels + panels // self.group

    def level(self, count):
        pairs = jnp.clip((count + 1) // 2, self.low, self.cap // 2)
        return (pairs - self.low + self.step - 1) // self.step

    def fill(self, counts_ref, table_ref):
        levels = [self.level(counts_ref[self.first + h]) for h in range(self.panels)]
        kinds = len(self.sizes)
        tally = [sum((lv == k).astype(jnp.int32) for lv in levels) for k in range(kinds)]
        at = [jnp.int32(0)]
        for k in range(kinds - 1):
            at.append(at[k] + tally[k])
        for h, lv in enumerate(levels):
            spot = at[0]
            for k in range(1, kinds):
                spot = jnp.where(lv == k, at[k], spot)
            table_ref[spot] = jnp.int32(self.first + h)
            at = [a + (lv == k).astype(jnp.int32) for k, a in enumerate(at)]
        for g in range(self.panels // self.group):
            table_ref[self.panels + g] = self.level(counts_ref[table_ref[(g + 1) * self.group - 1]])


def opening():
    def body(out_ref):
        out_ref[...] = jnp.zeros_like(out_ref)

    return pl.pallas_call(
        body,
        out_shape=jax.ShapeDtypeStruct((8, 128), jnp.float32),
        out_specs=VMEM,
        cost_estimate=pl.CostEstimate(flops=1 << 35, transcendentals=0, bytes_accessed=4096),
        compiler_params=pltpu.CompilerParams(vmem_limit_bytes=1 << 20),
        name="opening",
    )()


def plan(kinds, counts, after):
    def body(*refs):
        for kind, counts_ref, table_ref in zip(kinds, refs, refs[len(kinds) + 1 :]):
            kind.fill(counts_ref, table_ref)

    return pl.pallas_call(
        body,
        out_shape=[jax.ShapeDtypeStruct((kind.entries,), jnp.int32) for kind in kinds],
        in_specs=[SMEM] * len(kinds) + [VMEM],
        out_specs=[SMEM] * len(kinds),
        cost_estimate=pl.CostEstimate(flops=1 << 10, transcendentals=0, bytes_accessed=4096),
        compiler_params=pltpu.CompilerParams(vmem_limit_bytes=1 << 20),
        name="plan",
    )(*counts, after)


def product(kind, xs, chunk_of, counts, lists, slots_first, table, tiles, name, outs, ready=None, share=False):
    _, _, block, width = tiles.shape
    panels, group = kind.panels, kind.group
    pieces = len(xs)
    rows = sum(lanes[0].shape[0] for lanes in xs)
    blocks = sum(x.shape[1] for x in xs[0]) // block
    part = rows // 4

    laid = jax.ShapeDtypeStruct((blocks, rows, block), jnp.bfloat16)
    operands = [x for lanes in xs for x in lanes] if ready is None else [ready]

    def lay_out(x_refs, x_all):
        col = lax.axis_index("col")
        grouped = [[x_refs.pop(0) for _ in lanes] for lanes in xs]
        for t in range(4):
            flip = chunk_of(t) ^ col
            spot = (flip & 1) * 2 + flip // 2
            at = pl.ds(pl.multiple_of(spot * part, 16), part)
            lead = slice(0, part) if pieces == 4 else slice(t * part, (t + 1) * part)
            b = 0
            for ref in grouped[t if pieces == 4 else 0]:
                for lo in range(0, ref.shape[1], block):
                    x_all[b, at, :] = ref[lead, lo : lo + block]
                    b += 1

    def body(counts_ref, lists_ref, table_ref, *rest):
        if ready is None:
            x_refs = list(rest[: -2 - len(outs)])
            tiles_ref, x_all = rest[-2 - len(outs)], rest[-1]
            out_refs = rest[-1 - len(outs) : -1]
            lay_out(x_refs, x_all)
        else:
            x_all, tiles_ref, *out_refs = rest

        @pl.loop(0, panels // group)
        def _(g):
            level = table_ref[panels + g]
            members = [table_ref[g * group + u] for u in range(group)]
            for k, pairs in enumerate(kind.sizes):

                @pl.when(level == k)
                def _(pairs=pairs):
                    for panel in members:
                        count = counts_ref[panel]
                        chosen = []
                        for s in range(2 * pairs):
                            x = x_all[lists_ref[s, 0, panel] if slots_first else lists_ref[panel, 0, s]]
                            if s >= kind.least:
                                x = jnp.where(count > s, x, jnp.zeros_like(x))
                            chosen.append(x)
                        lhs = jnp.concatenate(chosen, axis=1)
                        rhs = tiles_ref[panel, : 2 * pairs].reshape(2 * pairs * block, width)
                        sums = jnp.dot(lhs, rhs, preferred_element_type=jnp.float32)
                        lanes = pl.ds(pl.multiple_of((panel - kind.first) * width, width), width)
                        at = 0
                        for out_ref in out_refs:
                            size = out_ref.shape[0]
                            out_ref[:, lanes] = sums[at : at + size].astype(out_ref.dtype)
                            at += size

    return pl.pallas_call(
        body,
        out_shape=[jax.ShapeDtypeStruct((n * part, panels * width), dtype) for n, dtype in outs] + [laid] * share,
        in_specs=[SMEM] * 3 + [VMEM] * (len(operands) + 1),
        out_specs=[VMEM] * (len(outs) + share),
        scratch_shapes=[] if share or ready is not None else [pltpu.VMEM(laid.shape, laid.dtype)],
        compiler_params=pltpu.CompilerParams(vmem_limit_bytes=(4 << 20) + rows * blocks * block * 4 + rows * width * 8),
        cost_estimate=pl.CostEstimate(flops=2 * rows * panels * tiles[0].size, transcendentals=0, bytes_accessed=panels * tiles[0].size * 2),
        name=name,
    )(counts, lists, table, *operands, tiles)


def elementwise(body, shapes, name, *args):
    return pl.pallas_call(
        body,
        out_shape=shapes,
        in_specs=[VMEM] * len(args),
        out_specs=[VMEM] * len(shapes),
        compiler_params=pltpu.CompilerParams(vmem_limit_bytes=4 << 20),
        name=name,
    )(*args)


def add_halves(kept, got):
    half, width = kept.shape[0] // 2, kept.shape[1]

    def body(kept_ref, got_ref, own_ref, send_ref):
        own_ref[...] = kept_ref[:half] + got_ref[:half].astype(jnp.float32)
        send_ref[...] = (kept_ref[half:] + got_ref[half:].astype(jnp.float32)).astype(jnp.bfloat16)

    shapes = [jax.ShapeDtypeStruct((half, width), jnp.float32), jax.ShapeDtypeStruct((half, width), jnp.bfloat16)]
    return elementwise(body, shapes, "add_halves", kept, got)


def swiglu(own, got, block, ahead=None):
    part, width = own.shape
    lead = 0 if ahead is None else ahead.shape[1]

    def body(own_ref, got_ref, *rest):
        for lo in range(0, width, 2 * block):
            gate = own_ref[:, lo : lo + block] + got_ref[:, lo : lo + block].astype(jnp.float32)
            up = own_ref[:, lo + block : lo + 2 * block] + got_ref[:, lo + block : lo + 2 * block].astype(jnp.float32)
            units = (gate / (1.0 + jnp.exp(-gate)) * up).astype(jnp.bfloat16)
            if lead:
                rest[1][:, lo // 2 : lo // 2 + block] = units
                rest[2][:, lead + lo // 2 : lead + lo // 2 + block] = units
            else:
                rest[0][:, lo // 2 : lo // 2 + block] = units
        if lead:
            rest[2][:, :lead] = rest[0][...]

    shapes = [jax.ShapeDtypeStruct((part, width // 2), jnp.bfloat16)]
    if lead:
        return elementwise(body, shapes + [jax.ShapeDtypeStruct((part, lead + width // 2), jnp.bfloat16)], "swiglu", own, got, ahead)
    return elementwise(body, shapes, "swiglu", own, got)[0]


def last_sum(own, *got):
    def body(own_ref, *rest):
        total = own_ref[...]
        for got_ref in rest[:-1]:
            total = total + got_ref[...].astype(jnp.float32)
        rest[-1][...] = total.astype(jnp.bfloat16)

    return elementwise(body, [jax.ShapeDtypeStruct(own.shape, jnp.bfloat16)], "last_sum", own, *got)[0]


def flipped(x, bit):
    return lax.ppermute(x, "col", [(i, i ^ bit) for i in range(4)])


def local(tokens, gate_tiles, gate_lists, gate_counts, down_tiles, down_lists, down_counts):
    cols, rows = lax.axis_size("col"), lax.axis_size("row")
    assert cols == 4
    block = gate_tiles.shape[3]
    total = tokens.shape[0] * rows
    part = total // cols
    square = rows == cols

    halves = 2 if gate_tiles.shape[0] % 2 == 0 else 1
    each = gate_tiles.shape[0] // halves
    gate_kinds = [Panels(i * each, each, gate_tiles.shape[2], 4, 1) for i in range(halves)]
    down_kind = Panels(0, down_tiles.shape[0], down_tiles.shape[2], 8, 2)
    gate_used, down_used = gate_counts.reshape(-1), down_counts.reshape(-1)
    slots = jnp.transpose(gate_lists, (2, 1, 0))

    def chunk_of(k):
        return lax.rem(lax.axis_index("row") + (rows - k), rows) if square else k

    tokens, opened = lax.optimization_barrier((tokens, opening()))
    if square:
        xs = [[tokens]] + [[lax.ppermute(tokens, "row", [(i, (i + k) % rows) for i in range(rows)])] for k in range(1, rows)]
    else:
        xs = [[lax.all_gather(tokens, "row", axis=0, tiled=True)]]
    *gate_tables, down_table = plan([*gate_kinds, down_kind], [gate_used] * halves + [down_used], opened)

    pairwise = [(2, jnp.float32), (2, jnp.bfloat16)]
    sums = []
    laid = None
    for kind, table in zip(gate_kinds, gate_tables):
        first = laid is None
        got = product(
            kind, xs, chunk_of, gate_used, slots, True, table, gate_tiles[:, 0], "gate_up", pairwise, ready=laid, share=first
        )
        sums.append((got[0], got[1]))
        laid = got[2] if first else laid
    pairs = []
    for kept, sent in sums:
        summed, crossing = add_halves(kept, flipped(sent, 1))
        pairs.append((summed, flipped(crossing, 2)))
    hidden = swiglu(*pairs[0], block)
    if len(pairs) > 1:
        first = hidden
        second, hidden = swiglu(*pairs[1], block, first)

    if square:

        def spread(x, k):
            there = [(r * cols + c, ((c + k) % rows) * cols + r) for r in range(rows) for c in range(cols)]
            return lax.ppermute(x, ("row", "col"), there)

        early = EARLY if len(pairs) > 1 else ()
        hs = [[spread(first, k), spread(second, k)] if k in early else [spread(hidden, k)] for k in range(cols)]
    else:
        every = lax.all_gather(hidden, "row", axis=1, tiled=True).reshape(part, cols, -1)
        every = lax.all_to_all(every, "col", 1, 0, tiled=True)
        hs = [[every.reshape(total, -1)]]
    straight = [(1, jnp.float32)] + [(1, jnp.bfloat16)] * 3
    own, *away = product(down_kind, hs, chunk_of, down_used, down_lists, False, down_table, down_tiles[:, 0], "down", straight)
    return last_sum(own, *[flipped(x, bit) for x, bit in zip(away, (2, 1, 3))])


def solution(mesh):
    return jax.shard_map(
        local,
        mesh=mesh,
        in_specs=(
            P(("groups", "row"), "col"),
            P(("groups", "row"), "col", None, None, None),
            P(("groups", "row"), "col", None),
            P(("groups", "row"), "col"),
            P(("groups", "row"), "col", None, None, None),
            P(("groups", "row"), "col", None),
            P(("groups", "row"), "col"),
        ),
        out_specs=P(("groups", "col"), "row"),
        check_vma=False,
    )
```
